32 devices in a mesh: groups: 2 (over y), block: 16 (over z, x, core).
Axes of the slice: x: 2, y: 2, z: 4, core: 2. Of those that a mesh axis runs over, the one named last changes fastest.
Arguments:
- queries: bfloat16 [49152, 1024], P(('groups', 'block')), parts along dimension 0, may hold values from -6 to 6
- keys: bfloat16 [49152, 1024], P(('groups', 'block')), parts along dimension 0, may hold values from -16 to 16
- values: bfloat16 [49152, 1024], P(('groups', 'block')), parts along dimension 0, may hold values from -12 to 12
Outputs:
- attended: bfloat16 [49152, 1024], P(('groups', 'block')), parts along dimension 0
The draws below stay inside these ranges and needn't reach their ends.
There are 2 independent parts, one for each index of `groups`. The reference program is written for one: setup_inputs(seed, part) draws one part's arguments, and reference() takes and returns one part's arrays. A program takes and returns all parts, laid end to end along the dimension named above; each array names one. Nothing has to cross between parts.
All inputs are finite; a program needn't handle non-finite values.
Results may differ from the reference program's by a relative error of at most 0.0029.
Values sent between devices are 32-bit elements; how exact they have to be, the bound alone decides.
No kernel may reach another device: no remote copies, remote signals or barrier semaphores. Data moves between devices by JAX's collectives and lax.ppermute only.
A program may use at most 128 MiB of HBM per device.

```python
import jax
import jax.numpy as jnp
from jax import lax

HEADS = 8
HEAD_DIM = 128
SPAN = 128
TOKENS = 24576
HD = 1024


def one_order(key):
    return jax.random.permutation(key, HEAD_DIM)


def shared_offsets(key):
    count = TOKENS // SPAN
    offset_key, order_key = jax.random.split(jax.random.fold_in(key, 5))
    offsets = 3.0 * jax.random.normal(offset_key, (count, 1, HEADS, HEAD_DIM), jnp.float32)
    orders = jax.vmap(one_order)(jax.random.split(order_key, HEADS))
    paired = jnp.take_along_axis(offsets, orders[None, None], axis=-1)
    return (offsets, paired)


def draw_keys(key, part):
    count = TOKENS // SPAN
    base_key, scale_key = jax.random.split(jax.random.fold_in(key, 11))
    base = jax.random.normal(base_key, (count, SPAN, HEADS, HEAD_DIM), jnp.float32)
    scales = jnp.exp(jax.random.uniform(scale_key, (count, 1, HEADS, 1), jnp.float32, -1.2, 1.2))
    offsets, paired = shared_offsets(key)
    keys = (base * scales + offsets).reshape(TOKENS, HEADS * HEAD_DIM)
    return jnp.clip(keys, -16.0, 16.0).astype(jnp.bfloat16)


def draw_values(key, part):
    count = TOKENS // SPAN
    base_key, shift_key = jax.random.split(jax.random.fold_in(key, 23))
    base = jax.random.normal(base_key, (count, SPAN, HEADS, HEAD_DIM), jnp.float32)
    shifts = jax.random.normal(shift_key, (count, 1, HEADS, HEAD_DIM), jnp.float32)
    offsets, paired = shared_offsets(key)
    values = (base + shifts + 0.5 * paired).reshape(TOKENS, HEADS * HEAD_DIM)
    return jnp.clip(values, -12.0, 12.0).astype(jnp.bfloat16)


def block_levels(rng, dims, pieces, low, top_value):
    level = 1.0
    for axis_at, blocks in pieces:
        heights = jax.random.uniform(jax.random.fold_in(jax.random.fold_in(rng, 6), axis_at), (blocks,), jnp.float32, low / len(pieces), top_value / len(pieces))
        level = level * jnp.repeat(jnp.exp(heights), dims[axis_at] // blocks).reshape((-1,) + (1,) * (len(dims) - 1 - axis_at))
    return level


def scatter_about(stream_key, extent, width, reach, cuts=(), kind=jnp.bfloat16):
    entries = jax.random.normal(stream_key, extent, jnp.float32) * width
    if len(cuts) > 0:
        entries = block_levels(stream_key, extent, cuts, -0.22, 0.18) * entries
    return jnp.clip(entries, min=-reach, max=reach).astype(kind)


def setup_inputs(seed: int = 0, part: int = 0) -> dict:
    splits = jax.random.split(jax.random.key(seed), 4)
    own_keys = jax.random.split(jax.random.fold_in(splits[3], part), 4)
    return {
        "queries": scatter_about(own_keys[0], (TOKENS, HD), 1.0, 6.0, ((0, 16),)),
        "keys": draw_keys(jax.random.fold_in(jax.random.fold_in(splits[3], part), 71), part),
        "values": draw_values(jax.random.fold_in(jax.random.fold_in(splits[3], part), 71), part),
    }


def features(x):
    return lax.optimization_barrier((jax.nn.elu(x.astype(jnp.float32)) + 1.0).astype(jnp.bfloat16)).astype(jnp.float32)


def reference(queries, keys, values):
    count = TOKENS // SPAN
    fq = features(queries).reshape(count, SPAN, HEADS, HEAD_DIM)
    fk = features(keys).reshape(count, SPAN, HEADS, HEAD_DIM)
    vv = values.astype(jnp.float32).reshape(count, SPAN, HEADS, HEAD_DIM)
    causal = jnp.arange(SPAN)[:, None] >= jnp.arange(SPAN)[None, :]

    def step(carry, inputs):
        state, norm = carry
        qc, kc, vc = inputs
        state_b = lax.optimization_barrier(state.astype(jnp.bfloat16)).astype(jnp.float32)
        inter = jnp.einsum('chd,hde->che', qc, state_b)
        den_inter = jnp.einsum('chd,hd->ch', qc, norm)
        scores = jnp.einsum('chd,khd->hck', qc, kc)
        scores = jnp.where(causal[None], scores, jnp.float32(0.0))
        scores_b = lax.optimization_barrier(scores.astype(jnp.bfloat16)).astype(jnp.float32)
        intra = jnp.einsum('hck,khe->che', scores_b, vc)
        den = den_inter + jnp.transpose(jnp.sum(scores, axis=-1), (1, 0))
        out = ((inter + intra) / den[..., None]).astype(jnp.bfloat16)
        state = state + jnp.einsum('chd,che->hde', kc, vc)
        norm = norm + jnp.sum(kc, axis=0)
        return (state, norm), out

    start = (jnp.zeros((HEADS, HEAD_DIM, HEAD_DIM), jnp.float32), jnp.zeros((HEADS, HEAD_DIM), jnp.float32))
    final, outs = lax.scan(step, start, (fq, fk, vv))
    return outs.reshape(TOKENS, HEADS * HEAD_DIM)
```

```python
import functools

import jax
import jax.numpy as jnp
from jax import lax
from jax.experimental import pallas as pl
from jax.experimental.pallas import tpu as pltpu
from jax.sharding import PartitionSpec as P

HEADS = 8
HEAD_DIM = 128
SPAN = 128
HALF = HEADS // 2
PIECE = HEAD_DIM + 8

VM = pl.BlockSpec(memory_space=pltpu.VMEM)
SM = pl.BlockSpec(memory_space=pltpu.SMEM)
ANY = pl.BlockSpec(memory_space=pl.ANY)
HBM = pl.BlockSpec(memory_space=pltpu.HBM)


def place():
    me = lax.axis_index("block")
    return me & 1, (me >> 1) & 3, me >> 3


def head_columns(j):
    core, local, group = place()
    half = (1 - core) if j < HALF else core
    head = half * HALF + ((j % HALF) ^ local)
    return pl.ds(pl.multiple_of(head * HEAD_DIM, HEAD_DIM), HEAD_DIM)


def features(x):
    x = x.astype(jnp.float32)
    return jnp.where(x > 0, x + 1.0, jnp.exp(x)).astype(jnp.bfloat16)


def key_states(count, first, k_ref, v_ref, fk_ref, pf_ref, nf_ref, t_ref, s):
    j = first + s
    acc = jnp.zeros((HEAD_DIM, HEAD_DIM), jnp.float32)
    norm = jnp.zeros((1, HEAD_DIM), jnp.float32)
    for c in range(count):
        rows = pl.ds(c * SPAN, SPAN)
        fk = features(k_ref[j, rows, :])
        fk_ref[s, rows, :] = fk
        pf_ref[s, rows, :] = acc
        nf_ref[s, pl.ds(c, 1), :] = norm
        acc = acc + lax.dot_general(
            fk, v_ref[j, rows, :], (((0,), (0,)), ((), ())), preferred_element_type=jnp.float32
        )
        norm = norm + jnp.sum(fk.astype(jnp.float32), axis=0, keepdims=True)
    t_ref[s, pl.ds(0, HEAD_DIM), :] = acc
    t_ref[s, pl.ds(HEAD_DIM, 8), :] = jnp.broadcast_to(norm, (8, HEAD_DIM))


def pre_a(count, k_hbm, v_hbm, k_ref, v_ref, fk_ref, pf_ref, nf_ref, t_ref, sems):
    copies = []
    for j in range(HEADS):
        cols = head_columns(j)
        ck = pltpu.make_async_copy(k_hbm.at[:, cols], k_ref.at[j], sems.at[0, j])
        cv = pltpu.make_async_copy(v_hbm.at[:, cols], v_ref.at[j], sems.at[1, j])
        ck.start()
        cv.start()
        copies.append((ck, cv))
    for j in range(HALF):
        copies[j][0].wait()
        copies[j][1].wait()
        key_states(count, 0, k_ref, v_ref, fk_ref, pf_ref, nf_ref, t_ref, j)
    for j in range(HALF, HEADS):
        copies[j][0].wait()
        copies[j][1].wait()


def pre_b(count, k_ref, v_ref, fk_ref, pf_ref, nf_ref, t_ref):
    for s in range(HALF):
        key_states(count, HALF, k_ref, v_ref, fk_ref, pf_ref, nf_ref, t_ref, s)


def mid(count, first, q_ref, fk_ref, nf_ref, fqs_ref, den_ref):
    causal = lax.broadcasted_iota(jnp.int32, (SPAN, SPAN), 0) >= lax.broadcasted_iota(
        jnp.int32, (SPAN, SPAN), 1
    )
    for s in range(HALF):
        cols = head_columns(first + s)
        for c in range(count):
            rows = pl.ds(c * SPAN, SPAN)
            fq = features(q_ref[rows, cols])
            scores = lax.dot_general(
                fq, fk_ref[s, rows, :], (((1,), (1,)), ((), ())), preferred_element_type=jnp.float32
            )
            scores = jnp.where(causal, scores, 0.0)
            den = jnp.sum(
                scores + fq.astype(jnp.float32) * nf_ref[s, pl.ds(c, 1), :], axis=-1, keepdims=True
            )
            fqs_ref[s, rows, pl.ds(0, HEAD_DIM)] = fq
            fqs_ref[s, rows, pl.ds(HEAD_DIM, SPAN)] = scores.astype(jnp.bfloat16)
            den_ref[s, rows, :] = jnp.broadcast_to(den, (SPAN, HEAD_DIM))


def post(count, first, fqs_ref, den_ref, pf_ref, v_ref, b_ref, *rest):
    o_hbm, o_ref, sems = rest[-3:]
    copies = []
    for s in range(HALF):
        before = b_ref[s, pl.ds(0, HEAD_DIM), :]
        before_norm = b_ref[s, pl.ds(HEAD_DIM, 1), :]
        for c in range(count):
            rows = pl.ds(c * SPAN, SPAN)
            fqs = fqs_ref[s, rows, :]
            prior = (pf_ref[s, rows, :] + before).astype(jnp.bfloat16)
            num = jnp.dot(
                fqs,
                jnp.concatenate([prior, v_ref[first + s, rows, :]], axis=0),
                preferred_element_type=jnp.float32,
            )
            fq = fqs[:, :HEAD_DIM].astype(jnp.float32)
            den = den_ref[s, rows, :] + jnp.sum(fq * before_norm, axis=-1, keepdims=True)
            o_ref[s, rows, :] = (num / den).astype(jnp.bfloat16)
        cols = head_columns(first + s)
        copy = pltpu.make_async_copy(o_ref.at[s], o_hbm.at[:, cols], sems.at[s])
        copy.start()
        copies.append(copy)
    for copy in copies:
        copy.wait()


def add_totals(keep_ref, got_ref, *piece_refs):
    for s in range(HALF):
        piece_refs[s][...] = keep_ref[s] + got_ref[s]


def inside_group(p0, p1, p2, p3, e0, e1, e2, e3, total_ref):
    core, local, group = place()
    pieces = [p[...] for p in (p0, p1, p2, p3)]
    for s, e in enumerate((e0, e1, e2, e3)):
        acc = jnp.zeros((PIECE, HEAD_DIM), jnp.float32)
        for o in range(4):
            if o != s:
                acc = acc + jnp.where((local ^ o) < (local ^ s), pieces[o], 0.0)
        e[...] = acc
    total_ref[...] = (pieces[0] + pieces[1]) + (pieces[2] + pieces[3])


def across_groups(bit, e0, e1, e2, e3, total_ref, got_ref, f0, f1, f2, f3, sum_ref):
    core, local, group = place()
    got = got_ref[...]
    earlier = jnp.where((group & bit) != 0, got, 0.0)
    for e, f in zip((e0, e1, e2, e3), (f0, f1, f2, f3)):
        f[...] = e[...] + earlier
    sum_ref[...] = total_ref[...] + got


def both_cores(b0, b1, b2, b3, keep_ref, got_ref, mine_ref, send_ref):
    core, local, group = place()
    for s, b in enumerate((b0, b1, b2, b3)):
        before = b[...]
        mine_ref[s] = before + jnp.where(core == 1, got_ref[s], 0.0)
        send_ref[s] = before + jnp.where(core == 0, keep_ref[s], 0.0)


def per_device(queries, keys, values):
    rows = queries.shape[0]
    count = rows // SPAN
    devices_n = lax.axis_size("block")
    groups_n = devices_n // 8
    assert groups_n * 8 == devices_n and groups_n & (groups_n - 1) == 0

    params = pltpu.CompilerParams(vmem_limit_bytes=8 << 20)
    f32, bf16 = jnp.float32, jnp.bfloat16
    sds = jax.ShapeDtypeStruct
    state_shapes = (
        sds((HALF, rows, HEAD_DIM), bf16),
        sds((HALF, rows, HEAD_DIM), f32),
        sds((HALF, (count + 7) // 8 * 8, HEAD_DIM), f32),
        sds((HALF, PIECE, HEAD_DIM), f32),
    )
    half_flops = HALF * count * 2 * SPAN * HEAD_DIM * HEAD_DIM

    def swap(x, distance):
        return lax.ppermute(x, "block", [(i, i ^ distance) for i in range(devices_n)])

    k_vm, v_vm, fk_a, pf_a, nf_a, t_send = pl.pallas_call(
        functools.partial(pre_a, count),
        out_shape=(sds((HEADS, rows, HEAD_DIM), bf16),) * 2 + state_shapes,
        in_specs=[HBM, HBM],
        out_specs=(VM,) * 6,
        scratch_shapes=[pltpu.SemaphoreType.DMA((2, HEADS))],
        compiler_params=params,
        cost_estimate=pl.CostEstimate(flops=half_flops, bytes_accessed=8 << 20, transcendentals=0),
        name="pre_a",
    )(keys, values)
    t_got = swap(t_send, 1)
    fk_b, pf_b, nf_b, t_keep = pl.pallas_call(
        functools.partial(pre_b, count),
        out_shape=state_shapes,
        in_specs=[VM, VM],
        out_specs=(VM,) * 4,
        compiler_params=params,
        cost_estimate=pl.CostEstimate(flops=half_flops, bytes_accessed=8 << 20, transcendentals=0),
        name="pre_b",
    )(k_vm, v_vm)

    def mid_call(first, fk, nf):
        return pl.pallas_call(
            functools.partial(mid, count, first),
            out_shape=(
                sds((HALF, rows, 2 * HEAD_DIM), bf16),
                sds((HALF, rows, HEAD_DIM), f32),
            ),
            in_specs=[VM, VM, VM],
            out_specs=(VM, VM),
            compiler_params=params,
            cost_estimate=pl.CostEstimate(flops=half_flops, bytes_accessed=8 << 20, transcendentals=0),
            name=f"mid_{first}",
        )(queries, fk, nf)

    piece = sds((PIECE, HEAD_DIM), f32)
    four = sds((HALF, PIECE, HEAD_DIM), f32)

    def small(kernel, name, ins, outs):
        return pl.pallas_call(
            kernel,
            out_shape=outs,
            in_specs=[VM] * len(ins),
            out_specs=(VM,) * len(outs),
            compiler_params=params,
            cost_estimate=pl.CostEstimate(flops=1 << 20, bytes_accessed=1 << 19, transcendentals=0),
            name=name,
        )(*ins)

    pieces = small(add_totals, "add_totals", (t_keep, t_got), (piece,) * 4)
    landed = {s: swap(pieces[s], 2 * s) for s in (3, 1, 2)}
    *finals, total = small(
        inside_group, "inside_group", (pieces[0], landed[1], landed[2], landed[3]), (piece,) * 5
    )
    bit = 1
    while bit < groups_n:
        got = swap(total, 8 * bit)
        *finals, total = small(
            functools.partial(across_groups, bit), f"across_{bit}", (*finals, total, got), (piece,) * 5
        )
        bit *= 2
    back = {s: swap(finals[s], 2 * s) for s in (3, 1, 2)}
    before_b, send_a = small(
        both_cores,
        "both_cores",
        (finals[0], back[1], back[2], back[3], t_keep, t_got),
        (four, four),
    )
    before_a = swap(send_a, 1)

    fqs_b, den_b = mid_call(HALF, fk_b, nf_b)
    fqs_a, den_a = mid_call(0, fk_a, nf_a)

    def post_call(first, fqs, den, pf, b, out=None):
        extra = () if out is None else (out,)
        return pl.pallas_call(
            functools.partial(post, count, first),
            out_shape=sds((rows, HEADS * HEAD_DIM), bf16),
            in_specs=[VM] * 5 + [HBM] * len(extra),
            out_specs=HBM,
            scratch_shapes=[
                pltpu.VMEM((HALF, rows, HEAD_DIM), bf16),
                pltpu.SemaphoreType.DMA((HALF,)),
            ],
            input_output_aliases={5: 0} if extra else {},
            compiler_params=params,
            cost_estimate=pl.CostEstimate(flops=half_flops * 2, bytes_accessed=8 << 20, transcendentals=0),
            name=f"post_{first}",
        )(fqs, den, pf, v_vm, b, *extra)

    out = post_call(HALF, fqs_b, den_b, pf_b, before_b)
    return post_call(0, fqs_a, den_a, pf_a, before_a, out)


def solution(mesh):
    placed = P(("groups", "block"), None)
    return jax.shard_map(
        per_device,
        mesh=mesh,
        in_specs=(placed, placed, placed),
        out_specs=placed,
        check_vma=False,
    )
```

```python
import functools

import jax
import jax.numpy as jnp
from jax import lax
from jax.experimental import pallas as pl
from jax.experimental.pallas import tpu as pltpu
from jax.sharding import PartitionSpec as P


HEADS = 8
HEAD_DIM = 128
SPAN = 128
HALF = HEADS // 2
PIECE = HEAD_DIM + 8
OFFSETS = ((0, 1, 2, 3), (0, 2, 3, 1))

VM = pl.BlockSpec(memory_space=pltpu.VMEM)
HBM = pl.BlockSpec(memory_space=pltpu.HBM)


def place():
    me = lax.axis_index("block")
    return me & 1, (me >> 1) & 3, me >> 3


def offset_of(core, slot):
    return jnp.where(core == 0, OFFSETS[0][slot], OFFSETS[1][slot])


def head_columns(mine, slot):
    core, local, _ = place()
    core = core if mine else 1 - core
    head = core * HALF + (offset_of(core, slot) ^ local)
    return pl.ds(pl.multiple_of(head * HEAD_DIM, HEAD_DIM), HEAD_DIM)


def features(x):
    x = x.astype(jnp.float32)
    return jnp.where(x > 0, x + 1.0, jnp.exp(x)).astype(jnp.bfloat16)


def key_states(count, k_ref, v_ref, fk_ref, pf_ref, nf_ref, t_ref):
    acc = jnp.zeros((HEAD_DIM, HEAD_DIM), jnp.float32)
    norm = jnp.zeros((1, HEAD_DIM), jnp.float32)
    for c in range(count):
        rows = pl.ds(c * SPAN, SPAN)
        fk = features(k_ref[rows, :])
        fk_ref[rows, :] = fk
        pf_ref[rows, :] = acc
        nf_ref[pl.ds(c, 1), :] = norm
        acc = acc + lax.dot_general(
            fk, v_ref[rows, :], (((0,), (0,)), ((), ())), preferred_element_type=jnp.float32
        )
        norm = norm + jnp.sum(fk.astype(jnp.float32), axis=0, keepdims=True)
    t_ref[pl.ds(0, HEAD_DIM), :] = acc
    t_ref[pl.ds(HEAD_DIM, 8), :] = jnp.broadcast_to(norm, (8, HEAD_DIM))


def pre_a(count, k_hbm, v_hbm, k_ref, v_ref, fk_ref, pf_ref, nf_ref, t_ref, sems):
    copies = []
    for j in range(HEADS):
        cols = head_columns(j >= HALF, j % HALF)
        ck = pltpu.make_async_copy(k_hbm.at[:, cols], k_ref.at[j], sems.at[0, j])
        cv = pltpu.make_async_copy(v_hbm.at[:, cols], v_ref.at[j], sems.at[1, j])
        ck.start()
        cv.start()
        copies.append((ck, cv))
    for j in range(HALF):
        copies[j][0].wait()
        copies[j][1].wait()
        key_states(
            count, k_ref.at[j], v_ref.at[j], fk_ref.at[j], pf_ref.at[j], nf_ref.at[j], t_ref.at[j]
        )
    for j in range(HALF, HEADS):
        copies[j][0].wait()
        copies[j][1].wait()


def pre_b(count, k_ref, v_ref, fk_ref, pf_ref, nf_ref, t_ref):
    for s in range(HALF):
        key_states(
            count,
            k_ref.at[HALF + s],
            v_ref.at[HALF + s],
            fk_ref.at[s],
            pf_ref.at[s],
            nf_ref.at[s],
            t_ref.at[s],
        )


def mid(count, mine, q_ref, fk_ref, nf_ref, fqs_ref, den_ref):
    causal = lax.broadcasted_iota(jnp.int32, (SPAN, SPAN), 0) >= lax.broadcasted_iota(
        jnp.int32, (SPAN, SPAN), 1
    )
    for s in range(HALF):
        cols = head_columns(mine, s)
        for c in range(count):
            rows = pl.ds(c * SPAN, SPAN)
            fq = features(q_ref[rows, cols])
            scores = lax.dot_general(
                fq, fk_ref[s, rows, :], (((1,), (1,)), ((), ())), preferred_element_type=jnp.float32
            )
            scores = jnp.where(causal, scores, 0.0)
            den = jnp.sum(
                scores + fq.astype(jnp.float32) * nf_ref[s, pl.ds(c, 1), :], axis=-1, keepdims=True
            )
            fqs_ref[s, rows, pl.ds(0, HEAD_DIM)] = fq
            fqs_ref[s, rows, pl.ds(HEAD_DIM, SPAN)] = scores.astype(jnp.bfloat16)
            den_ref[s, rows, :] = jnp.broadcast_to(den, (SPAN, HEAD_DIM))


def post(count, mine, slots, fqs_ref, den_ref, pf_ref, v_ref, b_ref, *rest):
    o_hbm, done_ref, o_ref, sems = rest[-4:]
    done_ref[...] = jnp.zeros_like(done_ref)
    first = HALF if mine else 0
    copies = []
    for i, s in enumerate(slots):
        before = b_ref[i, pl.ds(0, HEAD_DIM), :]
        before_norm = b_ref[i, pl.ds(HEAD_DIM, 1), :]
        for c in range(count):
            rows = pl.ds(c * SPAN, SPAN)
            fqs = fqs_ref[s, rows, :]
            prior = (pf_ref[s, rows, :] + before).astype(jnp.bfloat16)
            num = jnp.dot(
                fqs,
                jnp.concatenate([prior, v_ref[first + s, rows, :]], axis=0),
                preferred_element_type=jnp.float32,
            )
            fq = fqs[:, :HEAD_DIM].astype(jnp.float32)
            den = den_ref[s, rows, :] + jnp.sum(fq * before_norm, axis=-1, keepdims=True)
            o_ref[i, rows, :] = (num / den).astype(jnp.bfloat16)
        copy = pltpu.make_async_copy(o_ref.at[i], o_hbm.at[:, head_columns(mine, s)], sems.at[i])
        copy.start()
        copies.append(copy)
    for copy in copies:
        copy.wait()


def add_totals(keep_ref, got_ref, *piece_refs):
    for s in range(HALF):
        piece_refs[s][...] = keep_ref[s] + got_ref[s]


def inside_group(p0, p1, p2, p3, tied, e0, e1, e2, e3, total_ref):
    core, local, _ = place()
    pieces = [p[...] for p in (p0, p1, p2, p3)]
    chips = [local ^ offset_of(core, s) for s in range(4)]
    for s, e in enumerate((e0, e1, e2, e3)):
        acc = jnp.zeros((PIECE, HEAD_DIM), jnp.float32)
        for o in range(4):
            if o != s:
                acc = acc + jnp.where(chips[o] < chips[s], pieces[o], 0.0)
        e[...] = acc
    total_ref[...] = (pieces[0] + pieces[1]) + (pieces[2] + pieces[3])


def across_groups(bit, e0, e1, e2, e3, total_ref, got_ref, tied, f0, f1, f2, f3, sum_ref):
    _, _, group = place()
    got = got_ref[...]
    earlier = jnp.where((group & bit) != 0, got, 0.0)
    for e, f in zip((e0, e1, e2, e3), (f0, f1, f2, f3)):
        f[...] = e[...] + earlier
    sum_ref[...] = total_ref[...] + got


def both_cores(slots, *refs):
    n = len(slots)
    keep_ref, got_ref = refs[n : n + 2]
    mine_ref, send_ref = refs[-2:]
    core, _, _ = place()
    for i, s in enumerate(slots):
        before = refs[i][...]
        mine_ref[i] = before + jnp.where(core == 1, got_ref[s], 0.0)
        send_ref[i] = before + jnp.where(core == 0, keep_ref[s], 0.0)


def per_device(queries, keys, values):
    rows = queries.shape[0]
    count = rows // SPAN
    devices_n = lax.axis_size("block")
    groups_n = devices_n // 8
    assert groups_n * 8 == devices_n and groups_n & (groups_n - 1) == 0

    f32, bf16 = jnp.float32, jnp.bfloat16
    sds = jax.ShapeDtypeStruct
    state_shapes = (
        sds((HALF, rows, HEAD_DIM), bf16),
        sds((HALF, rows, HEAD_DIM), f32),
        sds((HALF, (count + 7) // 8 * 8, HEAD_DIM), f32),
        sds((HALF, PIECE, HEAD_DIM), f32),
    )
    half_flops = HALF * count * 2 * SPAN * HEAD_DIM * HEAD_DIM

    def call(kernel, ins, outs, in_specs=None, out_specs=None, grant=8, flops=half_flops, nbytes=8 << 20, **more):
        return pl.pallas_call(
            kernel,
            out_shape=outs,
            in_specs=in_specs or [VM] * len(ins),
            out_specs=out_specs or (VM,) * len(outs),
            compiler_params=pltpu.CompilerParams(vmem_limit_bytes=grant << 20),
            cost_estimate=pl.CostEstimate(flops=flops, bytes_accessed=nbytes, transcendentals=0),
            **more,
        )(*ins)

    def small(kernel, ins, outs):
        return call(kernel, ins, outs, flops=1 << 20, nbytes=1 << 19)

    def swap(x, distance):
        return lax.ppermute(x, "block", [(i, i ^ distance) for i in range(devices_n)])

    def swap_slot(x, slot):
        return lax.ppermute(
            x, "block", [(i, i ^ (2 * OFFSETS[i & 1][slot])) for i in range(devices_n)]
        )

    k_vm, v_vm, fk_a, pf_a, nf_a, t_send = call(
        functools.partial(pre_a, count),
        (keys, values),
        (sds((HEADS, rows, HEAD_DIM), bf16),) * 2 + state_shapes,
        in_specs=[HBM, HBM],
        grant=42,
        scratch_shapes=[pltpu.SemaphoreType.DMA((2, HEADS))],
    )
    t_got = swap(t_send, 1)
    fk_b, pf_b, nf_b, t_keep = call(functools.partial(pre_b, count), (k_vm, v_vm), state_shapes)

    def mid_call(mine, fk, nf):
        return call(
            functools.partial(mid, count, mine),
            (queries, fk, nf),
            (sds((HALF, rows, 2 * HEAD_DIM), bf16), sds((HALF, rows, HEAD_DIM), f32)),
        )

    piece = sds((PIECE, HEAD_DIM), f32)

    pieces = small(add_totals, (t_keep, t_got), (piece,) * 4)
    landed = {s: swap_slot(pieces[s], s) for s in (2, 3, 1)}
    fqs_b, den_b = mid_call(True, fk_b, nf_b)
    *finals, total = small(
        inside_group, (pieces[0], landed[1], landed[2], landed[3], den_b), (piece,) * 5
    )
    fqs_a, den_a = mid_call(False, fk_a, nf_a)
    bit = 1
    while bit < groups_n:
        got = swap(total, 8 * bit)
        *finals, total = small(
            functools.partial(across_groups, bit), (*finals, total, got, den_a), (piece,) * 5
        )
        bit *= 2
    back = {0: finals[0]}
    for s in (2, 3, 1):
        back[s] = swap_slot(finals[s], s)

    out = done = None
    for slots in ((0, 2), (3, 1)):
        two = sds((len(slots), PIECE, HEAD_DIM), f32)
        before_b, send_a = small(
            functools.partial(both_cores, slots),
            (*[back[s] for s in slots], t_keep, t_got, *([] if done is None else [done])),
            (two, two),
        )
        before_a = swap(send_a, 1)
        for mine, fqs, den, pf, b in (
            (True, fqs_b, den_b, pf_b, before_b),
            (False, fqs_a, den_a, pf_a, before_a),
        ):
            extra = () if out is None else (out,)
            out, done = call(
                functools.partial(post, count, mine, slots),
                (fqs, den, pf, v_vm, b, *extra),
                (sds((rows, HEADS * HEAD_DIM), bf16), sds((8, HEAD_DIM), f32)),
                in_specs=[VM] * 5 + [HBM] * len(extra),
                out_specs=(HBM, VM),
                scratch_shapes=[
                    pltpu.VMEM((len(slots), rows, HEAD_DIM), bf16),
                    pltpu.SemaphoreType.DMA((len(slots),)),
                ],
                input_output_aliases={5: 0} if extra else {},
            )
    return out


def solution(mesh):
    placed = P(("groups", "block"), None)

    return jax.shard_map(
        per_device,
        mesh=mesh,
        in_specs=(placed, placed, placed),
        out_specs=placed,
        check_vma=False,
    )
```

```python
import functools

import jax
import jax.numpy as jnp
from jax import lax
from jax.experimental import pallas as pl
from jax.experimental.pallas import tpu as pltpu
from jax.sharding import PartitionSpec as P


HEADS = 8
HEAD_DIM = 128
SPAN = 128
HALF = HEADS // 2
PIECE = HEAD_DIM + 8
OFFSETS = ((0, 1, 2, 3), (0, 2, 3, 1))

VM = pl.BlockSpec(memory_space=pltpu.VMEM)
HBM = pl.BlockSpec(memory_space=pltpu.HBM)


def place():
    me = lax.axis_index("block")
    return me & 1, (me >> 1) & 3, me >> 3


def offset_of(core, slot):
    return jnp.where(core == 0, OFFSETS[0][slot], OFFSETS[1][slot])


def head_columns(mine, slot):
    core, local, _ = place()
    core = core if mine else 1 - core
    head = core * HALF + (offset_of(core, slot) ^ local)
    return pl.ds(pl.multiple_of(head * HEAD_DIM, HEAD_DIM), HEAD_DIM)


def features(x):
    x = x.astype(jnp.float32)
    return jnp.where(x > 0, x + 1.0, jnp.exp(x)).astype(jnp.bfloat16)


def key_states(count, k_ref, v_ref, fk_ref, pf_ref, nf_ref, t_ref):
    acc = jnp.zeros((HEAD_DIM, HEAD_DIM), jnp.float32)
    norm = jnp.zeros((1, HEAD_DIM), jnp.float32)
    for c in range(count):
        rows = pl.ds(c * SPAN, SPAN)
        fk = features(k_ref[rows, :])
        fk_ref[rows, :] = fk
        pf_ref[rows, :] = acc
        nf_ref[pl.ds(c, 1), :] = norm
        acc = acc + lax.dot_general(
            fk, v_ref[rows, :], (((0,), (0,)), ((), ())), preferred_element_type=jnp.float32
        )
        norm = norm + jnp.sum(fk.astype(jnp.float32), axis=0, keepdims=True)
    t_ref[pl.ds(0, HEAD_DIM), :] = acc
    t_ref[pl.ds(HEAD_DIM, 8), :] = jnp.broadcast_to(norm, (8, HEAD_DIM))


def pre_a(count, early, k_hbm, v_hbm, k_ref, v_ref, *rest):
    *out_refs, sems = rest
    copies = []
    for j in range(HEADS):
        cols = head_columns(j >= HALF, j % HALF)
        ck = pltpu.make_async_copy(k_hbm.at[:, cols], k_ref.at[j], sems.at[0, j])
        cv = pltpu.make_async_copy(v_hbm.at[:, cols], v_ref.at[j], sems.at[1, j])
        ck.start()
        cv.start()
        copies.append((ck, cv))
    for j in range(HEADS):
        copies[j][0].wait()
        copies[j][1].wait()
        if j < HALF + early:
            at, outs = (j, out_refs[:4]) if j < HALF else (j - HALF, out_refs[4:])
            key_states(count, k_ref.at[j], v_ref.at[j], *(o.at[at] for o in outs))


def pre_b(count, early, k_ref, v_ref, *out_refs):
    for s in range(HALF - early):
        j = HALF + early + s
        key_states(count, k_ref.at[j], v_ref.at[j], *(o.at[s] for o in out_refs))


def pick(refs, slot):
    for ref in refs:
        if slot < ref.shape[0]:
            return ref.at[slot]
        slot -= ref.shape[0]


def mid(count, mine, parts, q_ref, *refs):
    fk_refs, nf_refs = refs[:parts], refs[parts : 2 * parts]
    fqs_ref, den_ref, done_ref = refs[2 * parts :]
    done_ref[...] = jnp.zeros_like(done_ref)
    causal = lax.broadcasted_iota(jnp.int32, (SPAN, SPAN), 0) >= lax.broadcasted_iota(
        jnp.int32, (SPAN, SPAN), 1
    )
    for s in range(HALF):
        cols = head_columns(mine, s)
        fk_ref, nf_ref = pick(fk_refs, s), pick(nf_refs, s)
        for c in range(count):
            rows = pl.ds(c * SPAN, SPAN)
            fq = features(q_ref[rows, cols])
            scores = lax.dot_general(
                fq, fk_ref[rows, :], (((1,), (1,)), ((), ())), preferred_element_type=jnp.float32
            )
            scores = jnp.where(causal, scores, 0.0)
            den = jnp.sum(
                scores + fq.astype(jnp.float32) * nf_ref[pl.ds(c, 1), :], axis=-1, keepdims=True
            )
            fqs_ref[s, rows, pl.ds(0, HEAD_DIM)] = fq
            fqs_ref[s, rows, pl.ds(HEAD_DIM, SPAN)] = scores.astype(jnp.bfloat16)
            den_ref[s, rows, :] = jnp.broadcast_to(den, (SPAN, HEAD_DIM))


def post(count, mine, parts, fqs_ref, den_ref, v_ref, b_ref, *rest):
    pf_refs = rest[:parts]
    o_hbm, o_ref, sems = rest[-3:]
    core, local, _ = place()
    core = core if mine else 1 - core
    width = HALF * HEAD_DIM
    half_cols = pl.ds(pl.multiple_of(core * width, width), width)
    first = HALF if mine else 0
    copies = []
    for c in range(count):
        rows = pl.ds(c * SPAN, SPAN)
        for s in range(HALF):
            fqs = fqs_ref[s, rows, :]
            prior = (pick(pf_refs, s)[rows, :] + b_ref[s, pl.ds(0, HEAD_DIM), :]).astype(
                jnp.bfloat16
            )
            num = jnp.dot(
                fqs,
                jnp.concatenate([prior, v_ref[first + s, rows, :]], axis=0),
                preferred_element_type=jnp.float32,
            )
            fq = fqs[:, :HEAD_DIM].astype(jnp.float32)
            den = den_ref[s, rows, :] + jnp.sum(
                fq * b_ref[s, pl.ds(HEAD_DIM, 1), :], axis=-1, keepdims=True
            )
            at = (offset_of(core, s) ^ local) * HEAD_DIM
            o_ref[rows, pl.ds(pl.multiple_of(at, HEAD_DIM), HEAD_DIM)] = (num / den).astype(
                jnp.bfloat16
            )
        copy = pltpu.make_async_copy(o_ref.at[rows, :], o_hbm.at[rows, half_cols], sems.at[c])
        copy.start()
        copies.append(copy)
    for copy in copies:
        copy.wait()


def add_totals(keep_parts, got_ref, *refs):
    keep_refs, piece_refs = refs[:keep_parts], refs[keep_parts:]
    for s in range(HALF):
        piece_refs[s][...] = pick(keep_refs, s)[...] + got_ref[s]


def inside_group(p0, p1, p2, p3, tied, e0, e1, e2, e3, total_ref):
    core, local, _ = place()
    pieces = [p[...] for p in (p0, p1, p2, p3)]
    chips = [local ^ offset_of(core, s) for s in range(4)]
    for s, e in enumerate((e0, e1, e2, e3)):
        acc = jnp.zeros((PIECE, HEAD_DIM), jnp.float32)
        for o in range(4):
            if o != s:
                acc = acc + jnp.where(chips[o] < chips[s], pieces[o], 0.0)
        e[...] = acc
    total_ref[...] = (pieces[0] + pieces[1]) + (pieces[2] + pieces[3])


def across_groups(bit, e0, e1, e2, e3, total_ref, got_ref, tied, f0, f1, f2, f3, *sum_ref):
    _, _, group = place()
    got = got_ref[...]
    earlier = jnp.where((group & bit) != 0, got, 0.0)
    for e, f in zip((e0, e1, e2, e3), (f0, f1, f2, f3)):
        f[...] = e[...] + earlier
    for ref in sum_ref:
        ref[...] = total_ref[...] + got


def both_cores(keep_parts, b0, b1, b2, b3, got_ref, *refs):
    keep_refs = refs[:keep_parts]
    mine_ref, send_ref = refs[keep_parts:]
    core, _, _ = place()
    for s, b in enumerate((b0, b1, b2, b3)):
        before = b[...]
        mine_ref[s] = before + jnp.where(core == 1, got_ref[s], 0.0)
        send_ref[s] = before + jnp.where(core == 0, pick(keep_refs, s)[...], 0.0)


def per_device(queries, keys, values):
    rows = queries.shape[0]
    count = rows // SPAN
    devices_n = lax.axis_size("block")
    groups_n = devices_n // 8
    assert groups_n * 8 == devices_n and groups_n & (groups_n - 1) == 0

    f32, bf16 = jnp.float32, jnp.bfloat16
    sds = jax.ShapeDtypeStruct

    def state_shapes(slots):
        return (
            sds((slots, rows, HEAD_DIM), bf16),
            sds((slots, rows, HEAD_DIM), f32),
            sds((slots, (count + 7) // 8 * 8, HEAD_DIM), f32),
            sds((slots, PIECE, HEAD_DIM), f32),
        )

    half_flops = HALF * count * 2 * SPAN * HEAD_DIM * HEAD_DIM

    def call(kernel, ins, outs, in_specs=None, out_specs=None, grant=8, flops=half_flops, nbytes=8 << 20, **more):
        return pl.pallas_call(
            kernel,
            out_shape=outs,
            in_specs=in_specs or [VM] * len(ins),
            out_specs=out_specs or (VM,) * len(outs),
            compiler_params=pltpu.CompilerParams(vmem_limit_bytes=grant << 20),
            cost_estimate=pl.CostEstimate(flops=flops, bytes_accessed=nbytes, transcendentals=0),
            **more,
        )(*ins)

    def small(kernel, ins, outs):
        return call(kernel, ins, outs, flops=1 << 20, nbytes=1 << 19)

    def swap(x, distance):
        return lax.ppermute(x, "block", [(i, i ^ distance) for i in range(devices_n)])

    def swap_slot(x, slot):
        return lax.ppermute(
            x, "block", [(i, i ^ (2 * OFFSETS[i & 1][slot])) for i in range(devices_n)]
        )

    early = 1
    k_vm, v_vm, *states = call(
        functools.partial(pre_a, count, early),
        (keys, values),
        (sds((HEADS, rows, HEAD_DIM), bf16),) * 2
        + state_shapes(HALF)
        + (state_shapes(early) if early else ()),
        in_specs=[HBM, HBM],
        grant=40,
        scratch_shapes=[pltpu.SemaphoreType.DMA((2, HEADS))],
    )
    fk_a, pf_a, nf_a, t_send = states[:4]
    t_got = swap(t_send, 1)
    late = call(functools.partial(pre_b, count, early), (k_vm, v_vm), state_shapes(HALF - early))
    fk_b, pf_b, nf_b, t_keep = ([x, y] for x, y in zip(states[4:], late)) if early else ([x] for x in late)

    def mid_call(mine, fk, nf):
        return call(
            functools.partial(mid, count, mine, len(fk)),
            (queries, *fk, *nf),
            (
                sds((HALF, rows, 2 * HEAD_DIM), bf16),
                sds((HALF, rows, HEAD_DIM), f32),
                sds((8, HEAD_DIM), f32),
            ),
        )

    piece = sds((PIECE, HEAD_DIM), f32)

    pieces = small(functools.partial(add_totals, len(t_keep)), (t_got, *t_keep), (piece,) * 4)
    landed = {}
    for s in (2, 3, 1):
        landed[s] = swap_slot(pieces[s], s)
    fqs_b, den_b, done_b = mid_call(True, fk_b, nf_b)
    *finals, total = small(
        inside_group, (pieces[0], landed[1], landed[2], landed[3], done_b), (piece,) * 5
    )
    fqs_a, den_a, done_a = mid_call(False, [fk_a], [nf_a])
    bit = 1
    while bit < groups_n:
        got = swap(total, 8 * bit)
        sums = 1 if 2 * bit < groups_n else 0
        finals = small(
            functools.partial(across_groups, bit),
            (*finals[:4], total, got, done_a),
            (piece,) * (4 + sums),
        )
        total = finals[-1]
        bit *= 2
    back = {0: finals[0]}
    for s in (2, 3, 1):
        back[s] = swap_slot(finals[s], s)
    four = sds((HALF, PIECE, HEAD_DIM), f32)
    before_b, send_a = small(
        functools.partial(both_cores, len(t_keep)),
        (back[0], back[1], back[2], back[3], t_got, *t_keep),
        (four, four),
    )
    before_a = swap(send_a, 1)

    out = None
    for mine, fqs, den, pf, b in (
        (True, fqs_b, den_b, pf_b, before_b),
        (False, fqs_a, den_a, [pf_a], before_a),
    ):
        ins = (fqs, den, v_vm, b, *pf)
        extra = () if out is None else (out,)
        out = call(
            functools.partial(post, count, mine, len(pf)),
            (*ins, *extra),
            sds((rows, HEADS * HEAD_DIM), bf16),
            in_specs=[VM] * len(ins) + [HBM] * len(extra),
            out_specs=HBM,
            scratch_shapes=[
                pltpu.VMEM((rows, HALF * HEAD_DIM), bf16),
                pltpu.SemaphoreType.DMA((count,)),
            ],
            input_output_aliases={len(ins): 0} if extra else {},
        )
    return out


def solution(mesh):
    placed = P(("groups", "block"), None)

    return jax.shard_map(
        per_device,
        mesh=mesh,
        in_specs=(placed, placed, placed),
        out_specs=placed,
        check_vma=False,
    )
```

```python
import functools

import jax
import jax.numpy as jnp
from jax import lax
from jax.experimental import pallas as pl
from jax.experimental.pallas import tpu as pltpu
from jax.sharding import PartitionSpec as P


HEADS = 8
HEAD_DIM = 128
SPAN = 128
HALF = HEADS // 2
PIECE = HEAD_DIM + 8
READS = 1
SLOT_ORDER = (3, 2, 1)

VM = pl.BlockSpec(memory_space=pltpu.VMEM)
HBM = pl.BlockSpec(memory_space=pltpu.HBM)


def place():
    me = lax.axis_index("block")
    return me & 1, (me >> 1) & 3, me >> 3


def head_columns(mine, slot):
    core, local, _ = place()
    core = core if mine else 1 - core
    head = core * HALF + (slot ^ local)
    return pl.ds(pl.multiple_of(head * HEAD_DIM, HEAD_DIM), HEAD_DIM)


def features(x):
    x = x.astype(jnp.float32)
    return jnp.where(x > 0, x + 1.0, jnp.exp(x)).astype(jnp.bfloat16)


def key_states(count, k_ref, v_ref, fk_ref, pf_ref, nf_ref, t_ref):
    acc = jnp.zeros((HEAD_DIM, HEAD_DIM), jnp.float32)
    norm = jnp.zeros((1, HEAD_DIM), jnp.float32)
    for c in range(count):
        rows = pl.ds(c * SPAN, SPAN)
        fk = features(k_ref[rows, :])
        fk_ref[rows, :] = fk
        pf_ref[rows, :] = acc
        nf_ref[pl.ds(c, 1), :] = norm
        acc = acc + lax.dot_general(
            fk, v_ref[rows, :], (((0,), (0,)), ((), ())), preferred_element_type=jnp.float32
        )
        norm = norm + jnp.sum(fk.astype(jnp.float32), axis=0, keepdims=True)
    t_ref[pl.ds(0, HEAD_DIM), :] = acc
    t_ref[pl.ds(HEAD_DIM, 8), :] = jnp.broadcast_to(norm, (8, HEAD_DIM))


def pre_a(count, k_hbm, v_hbm, k_ref, v_ref, *rest):
    *out_refs, sems = rest

    part = count * SPAN // READS

    def copies(j, i):
        cols = head_columns(j >= HALF, j % HALF)
        rows = pl.ds(i * part, part)
        return (
            pltpu.make_async_copy(k_hbm.at[rows, cols], k_ref.at[j, rows], sems.at[0, j, i]),
            pltpu.make_async_copy(v_hbm.at[rows, cols], v_ref.at[j, rows], sems.at[1, j, i]),
        )

    def each(j, act):
        for i in range(READS):
            for copy in copies(j, i):
                act(copy)

    for j in range(HEADS):
        each(j, lambda copy: copy.start())
    for j in range(HEADS):
        each(j, lambda copy: copy.wait())
        if j < HALF:
            key_states(count, k_ref.at[j], v_ref.at[j], *(o.at[j] for o in out_refs))


def pre_b(count, k_ref, v_ref, *out_refs):
    for s in range(HALF):
        key_states(count, k_ref.at[HALF + s], v_ref.at[HALF + s], *(o.at[s] for o in out_refs))


def queries_of(count, mine, q_ref, fk_ref, nf_ref, fqs_ref, den_ref):
    causal = lax.broadcasted_iota(jnp.int32, (SPAN, SPAN), 0) >= lax.broadcasted_iota(
        jnp.int32, (SPAN, SPAN), 1
    )
    for s in range(HALF):
        cols = head_columns(mine, s)
        for c in range(count):
            rows = pl.ds(c * SPAN, SPAN)
            fq = features(q_ref[rows, cols])
            scores = lax.dot_general(
                fq, fk_ref[s, rows, :], (((1,), (1,)), ((), ())), preferred_element_type=jnp.float32
            )
            scores = jnp.where(causal, scores, 0.0)
            den = jnp.sum(
                scores + fq.astype(jnp.float32) * nf_ref[s, pl.ds(c, 1), :], axis=-1, keepdims=True
            )
            fqs_ref[s, rows, pl.ds(0, HEAD_DIM)] = fq
            fqs_ref[s, rows, pl.ds(HEAD_DIM, SPAN)] = scores.astype(jnp.bfloat16)
            den_ref[s, rows, :] = jnp.broadcast_to(den, (SPAN, HEAD_DIM))


def mid_mine(count, q_ref, fk_ref, nf_ref, fqs_ref, den_ref, done_ref):
    done_ref[...] = jnp.zeros_like(done_ref)
    queries_of(count, True, q_ref, fk_ref, nf_ref, fqs_ref, den_ref)


def mid_other(count, q_ref, fk_ref, nf_ref, fqs_ref, den_ref, done_ref):
    done_ref[...] = jnp.zeros_like(done_ref)
    queries_of(count, False, q_ref, fk_ref, nf_ref, fqs_ref, den_ref)


def half_columns(mine):
    core, _, _ = place()
    width = HALF * HEAD_DIM
    return pl.ds(pl.multiple_of((core if mine else 1 - core) * width, width), width)


def attend(c, first, fqs_ref, den_ref, v_ref, b_ref, pf_ref, o_ref):
    _, local, _ = place()
    rows = pl.ds(c * SPAN, SPAN)
    for s in range(HALF):
        fqs = fqs_ref[s, rows, :]
        prior = (pf_ref[s, rows, :] + b_ref[s, pl.ds(0, HEAD_DIM), :]).astype(jnp.bfloat16)
        num = jnp.dot(
            fqs,
            jnp.concatenate([prior, v_ref[first + s, rows, :]], axis=0),
            preferred_element_type=jnp.float32,
        )
        fq = fqs[:, :HEAD_DIM].astype(jnp.float32)
        den = den_ref[s, rows, :] + jnp.sum(
            fq * b_ref[s, pl.ds(HEAD_DIM, 1), :], axis=-1, keepdims=True
        )
        at = (s ^ local) * HEAD_DIM
        o_ref[rows, pl.ds(pl.multiple_of(at, HEAD_DIM), HEAD_DIM)] = (num / den).astype(
            jnp.bfloat16
        )


def post_mine(count, fqs_ref, den_ref, v_ref, b_ref, pf_ref, o_ref):
    for c in range(count):
        attend(c, HALF, fqs_ref, den_ref, v_ref, b_ref, pf_ref, o_ref)


def post_other(count, fqs_ref, den_ref, v_ref, b_ref, pf_ref, mine_ref, o_hbm, o_ref, sems):
    def copy(c, mine):
        rows = pl.ds(c * SPAN, SPAN)
        return pltpu.make_async_copy(
            (mine_ref if mine else o_ref).at[rows, :],
            o_hbm.at[rows, half_columns(mine)],
            sems.at[int(mine), c],
        )

    for c in range(count):
        copy(c, True).start()
    for c in range(count):
        attend(c, 0, fqs_ref, den_ref, v_ref, b_ref, pf_ref, o_ref)
        copy(c, False).start()
    for c in range(count):
        copy(c, True).wait()
        copy(c, False).wait()


def add_totals(keep_ref, got_ref, *piece_refs):
    for s in range(HALF):
        piece_refs[s][...] = keep_ref[s] + got_ref[s]


def inside_group(p0, p1, p2, p3, tied, e0, e1, e2, e3, total_ref):
    _, local, _ = place()
    pieces = [p[...] for p in (p0, p1, p2, p3)]
    chips = [local ^ s for s in range(4)]
    for s, e in enumerate((e0, e1, e2, e3)):
        acc = jnp.zeros((PIECE, HEAD_DIM), jnp.float32)
        for o in range(4):
            if o != s:
                acc = acc + jnp.where(chips[o] < chips[s], pieces[o], 0.0)
        e[...] = acc
    total_ref[...] = (pieces[0] + pieces[1]) + (pieces[2] + pieces[3])


def across_groups(bit, e0, e1, e2, e3, total_ref, got_ref, tied, f0, f1, f2, f3, *sum_ref):
    _, _, group = place()
    got = got_ref[...]
    earlier = jnp.where((group & bit) != 0, got, 0.0)
    for e, f in zip((e0, e1, e2, e3), (f0, f1, f2, f3)):
        f[...] = e[...] + earlier
    for ref in sum_ref:
        ref[...] = total_ref[...] + got


def both_cores(b0, b1, b2, b3, keep_ref, got_ref, mine_ref, send_ref):
    core, _, _ = place()
    for s, b in enumerate((b0, b1, b2, b3)):
        before = b[...]
        mine_ref[s] = before + jnp.where(core == 1, got_ref[s], 0.0)
        send_ref[s] = before + jnp.where(core == 0, keep_ref[s], 0.0)


def per_device(queries, keys, values):
    rows = queries.shape[0]
    count = rows // SPAN
    devices_n = lax.axis_size("block")
    groups_n = devices_n // 8
    assert groups_n * 8 == devices_n and groups_n & (groups_n - 1) == 0

    f32, bf16 = jnp.float32, jnp.bfloat16
    sds = jax.ShapeDtypeStruct

    state_shapes = (
        sds((HALF, rows, HEAD_DIM), bf16),
        sds((HALF, rows, HEAD_DIM), f32),
        sds((HALF, (count + 7) // 8 * 8, HEAD_DIM), f32),
        sds((HALF, PIECE, HEAD_DIM), f32),
    )
    query_shapes = (
        sds((HALF, rows, 2 * HEAD_DIM), bf16),
        sds((HALF, rows, HEAD_DIM), f32),
    )
    token = sds((8, HEAD_DIM), f32)
    half_flops = HALF * count * 2 * SPAN * HEAD_DIM * HEAD_DIM

    def call(kernel, ins, outs, in_specs=None, out_specs=None, grant=8, flops=half_flops, nbytes=8 << 20, **more):
        return pl.pallas_call(
            kernel,
            out_shape=outs,
            in_specs=in_specs or [VM] * len(ins),
            out_specs=out_specs or (VM,) * len(outs),
            compiler_params=pltpu.CompilerParams(vmem_limit_bytes=grant << 20),
            cost_estimate=pl.CostEstimate(flops=flops, bytes_accessed=nbytes, transcendentals=0),
            **more,
        )(*ins)

    def small(kernel, ins, outs):
        return call(kernel, ins, outs, flops=1 << 20, nbytes=1 << 19)

    def swap(x, distance):
        return lax.ppermute(x, "block", [(i, i ^ distance) for i in range(devices_n)])

    def swap_slot(x, slot):
        return swap(x, 2 * slot)

    k_vm, v_vm, fk_a, pf_a, nf_a, t_send = call(
        functools.partial(pre_a, count),
        (keys, values),
        (sds((HEADS, rows, HEAD_DIM), bf16),) * 2 + state_shapes,
        in_specs=[HBM, HBM],
        grant=42,
        scratch_shapes=[pltpu.SemaphoreType.DMA((2, HEADS, READS))],
    )
    t_got = swap(t_send, 1)
    fk_b, pf_b, nf_b, t_keep = call(functools.partial(pre_b, count), (k_vm, v_vm), state_shapes)

    piece = sds((PIECE, HEAD_DIM), f32)

    pieces = small(add_totals, (t_keep, t_got), (piece,) * 4)
    landed = {}
    for s in SLOT_ORDER:
        landed[s] = swap_slot(pieces[s], s)
    fqs_b, den_b, done_b = call(
        functools.partial(mid_mine, count), (queries, fk_b, nf_b), (*query_shapes, token)
    )
    *finals, total = small(
        inside_group, (pieces[0], landed[1], landed[2], landed[3], done_b), (piece,) * 5
    )
    fqs_a, den_a, done_a = call(
        functools.partial(mid_other, count), (queries, fk_a, nf_a), (*query_shapes, token)
    )
    bit = 1
    while bit < groups_n:
        got = swap(total, 8 * bit)
        sums = 1 if 2 * bit < groups_n else 0
        finals = small(
            functools.partial(across_groups, bit),
            (*finals[:4], total, got, done_a),
            (piece,) * (4 + sums),
        )
        total = finals[-1]
        bit *= 2
    back = {0: finals[0]}
    for s in SLOT_ORDER:
        back[s] = swap_slot(finals[s], s)
    four = sds((HALF, PIECE, HEAD_DIM), f32)
    before_b, send_a = small(
        both_cores, (back[0], back[1], back[2], back[3], t_keep, t_got), (four, four)
    )
    before_a = swap(send_a, 1)

    (mine,) = call(
        functools.partial(post_mine, count),
        (fqs_b, den_b, v_vm, before_b, pf_b),
        (sds((rows, HALF * HEAD_DIM), bf16),),
    )
    return call(
        functools.partial(post_other, count),
        (fqs_a, den_a, v_vm, before_a, pf_a, mine),
        sds((rows, HEADS * HEAD_DIM), bf16),
        out_specs=HBM,
        scratch_shapes=[
            pltpu.VMEM((rows, HALF * HEAD_DIM), bf16),
            pltpu.SemaphoreType.DMA((2, count)),
        ],
    )


def solution(mesh):
    placed = P(("groups", "block"), None)

    return jax.shard_map(
        per_device,
        mesh=mesh,
        in_specs=(placed, placed, placed),
        out_specs=placed,
        check_vma=False,
    )
```

```python
import functools

import jax
import jax.numpy as jnp
from jax import lax
from jax.experimental import pallas as pl
from jax.experimental.pallas import tpu as pltpu
from jax.sharding import PartitionSpec as P


HEADS = 8
HEAD_DIM = 128
SPAN = 128
HALF = HEADS // 2
PIECE = HEAD_DIM + 8
READS = 1
SLOT_ORDER = (3, 2, 1)

VM = pl.BlockSpec(memory_space=pltpu.VMEM)
HBM = pl.BlockSpec(memory_space=pltpu.HBM)


def place():
    me = lax.axis_index("block")
    return me & 1, (me >> 1) & 3, me >> 3


def head_columns(mine, slot):
    core, local, _ = place()
    core = core if mine else 1 - core
    head = core * HALF + (slot ^ local)
    return pl.ds(pl.multiple_of(head * HEAD_DIM, HEAD_DIM), HEAD_DIM)


def features(x):
    x = x.astype(jnp.float32)
    return jnp.where(x > 0, x + 1.0, jnp.exp(x)).astype(jnp.bfloat16)


def key_states(count, k_ref, v_ref, fk_ref, pf_ref, nf_ref, t_ref):
    acc = jnp.zeros((HEAD_DIM, HEAD_DIM), jnp.float32)
    norm = jnp.zeros((1, HEAD_DIM), jnp.float32)
    for c in range(count):
        rows = pl.ds(c * SPAN, SPAN)
        fk = features(k_ref[rows, :])
        fk_ref[rows, :] = fk
        pf_ref[rows, :] = acc
        nf_ref[pl.ds(c, 1), :] = norm
        acc = acc + lax.dot_general(
            fk, v_ref[rows, :], (((0,), (0,)), ((), ())), preferred_element_type=jnp.float32
        )
        norm = norm + jnp.sum(fk.astype(jnp.float32), axis=0, keepdims=True)
    t_ref[pl.ds(0, HEAD_DIM), :] = acc
    t_ref[pl.ds(HEAD_DIM, 8), :] = jnp.broadcast_to(norm, (8, HEAD_DIM))


def pre_a(count, k_hbm, v_hbm, k_ref, v_ref, *rest):
    *out_refs, sems = rest

    part = count * SPAN // READS

    def copies(j, i):
        cols = head_columns(j >= HALF, j % HALF)
        rows = pl.ds(i * part, part)
        return (
            pltpu.make_async_copy(k_hbm.at[rows, cols], k_ref.at[j, rows], sems.at[0, j, i]),
            pltpu.make_async_copy(v_hbm.at[rows, cols], v_ref.at[j, rows], sems.at[1, j, i]),
        )

    def each(j, act):
        for i in range(READS):
            for copy in copies(j, i):
                act(copy)

    for j in range(HEADS):
        each(j, lambda copy: copy.start())
    for j in range(HEADS):
        each(j, lambda copy: copy.wait())
        if j < HALF:
            key_states(count, k_ref.at[j], v_ref.at[j], *(o.at[j] for o in out_refs))


def pre_b(count, k_ref, v_ref, *out_refs):
    for s in range(HALF):
        key_states(count, k_ref.at[HALF + s], v_ref.at[HALF + s], *(o.at[s] for o in out_refs))


def queries_of(count, mine, q_ref, fk_ref, nf_ref, fqs_ref, den_ref):
    causal = lax.broadcasted_iota(jnp.int32, (SPAN, SPAN), 0) >= lax.broadcasted_iota(
        jnp.int32, (SPAN, SPAN), 1
    )
    for s in range(HALF):
        cols = head_columns(mine, s)
        for c in range(count):
            rows = pl.ds(c * SPAN, SPAN)
            fq = features(q_ref[rows, cols])
            scores = lax.dot_general(
                fq, fk_ref[s, rows, :], (((1,), (1,)), ((), ())), preferred_element_type=jnp.float32
            )
            scores = jnp.where(causal, scores, 0.0)
            den = jnp.sum(
                scores + fq.astype(jnp.float32) * nf_ref[s, pl.ds(c, 1), :], axis=-1, keepdims=True
            )
            fqs_ref[s, rows, pl.ds(0, HEAD_DIM)] = fq
            fqs_ref[s, rows, pl.ds(HEAD_DIM, SPAN)] = scores.astype(jnp.bfloat16)
            den_ref[s, rows, :] = jnp.broadcast_to(den, (SPAN, HEAD_DIM))


def mid_mine(count, q_ref, fk_ref, nf_ref, fqs_ref, den_ref, done_ref):
    done_ref[...] = jnp.zeros_like(done_ref)
    queries_of(count, True, q_ref, fk_ref, nf_ref, fqs_ref, den_ref)


def mid_other(count, q_ref, fk_ref, nf_ref, fqs_ref, den_ref, done_ref):
    done_ref[...] = jnp.zeros_like(done_ref)
    queries_of(count, False, q_ref, fk_ref, nf_ref, fqs_ref, den_ref)


def half_columns(mine):
    core, _, _ = place()
    width = HALF * HEAD_DIM
    return pl.ds(pl.multiple_of((core if mine else 1 - core) * width, width), width)


def attend(c, first, fqs_ref, den_ref, v_ref, b_ref, pf_ref, o_ref, slots=range(HALF)):
    _, local, _ = place()
    rows = pl.ds(c * SPAN, SPAN)
    for s in slots:
        fqs = fqs_ref[s, rows, :]
        prior = (pf_ref[s, rows, :] + b_ref[s, pl.ds(0, HEAD_DIM), :]).astype(jnp.bfloat16)
        num = jnp.dot(
            fqs,
            jnp.concatenate([prior, v_ref[first + s, rows, :]], axis=0),
            preferred_element_type=jnp.float32,
        )
        fq = fqs[:, :HEAD_DIM].astype(jnp.float32)
        den = den_ref[s, rows, :] + jnp.sum(
            fq * b_ref[s, pl.ds(HEAD_DIM, 1), :], axis=-1, keepdims=True
        )
        at = (s ^ local) * HEAD_DIM
        o_ref[rows, pl.ds(pl.multiple_of(at, HEAD_DIM), HEAD_DIM)] = (num / den).astype(
            jnp.bfloat16
        )


def post_first(count, fqs_ref, den_ref, v_ref, final_ref, got_ref, pf_ref, o_ref, done_ref, b_ref):
    core, _, _ = place()
    done_ref[...] = jnp.zeros_like(done_ref)
    b_ref[0] = final_ref[...] + jnp.where(core == 1, got_ref[0], 0.0)
    for c in range(count):
        attend(c, HALF, fqs_ref, den_ref, v_ref, b_ref, pf_ref, o_ref, (0,))


def post_mine(count, fqs_ref, den_ref, v_ref, b_ref, pf_ref, first_ref, o_ref):
    for c in range(count):
        attend(c, HALF, fqs_ref, den_ref, v_ref, b_ref, pf_ref, o_ref, range(1, HALF))


def post_other(count, fqs_ref, den_ref, v_ref, b_ref, pf_ref, mine_ref, o_hbm, o_ref, sems):
    def copy(c, mine):
        rows = pl.ds(c * SPAN, SPAN)
        return pltpu.make_async_copy(
            (mine_ref if mine else o_ref).at[rows, :],
            o_hbm.at[rows, half_columns(mine)],
            sems.at[int(mine), c],
        )

    for c in range(count):
        copy(c, True).start()
    for c in range(count):
        attend(c, 0, fqs_ref, den_ref, v_ref, b_ref, pf_ref, o_ref)
        copy(c, False).start()
    for c in range(count):
        copy(c, True).wait()
        copy(c, False).wait()


def add_totals(keep_ref, got_ref, *piece_refs):
    for s in range(HALF):
        piece_refs[s][...] = keep_ref[s] + got_ref[s]


def inside_group(p0, p1, p2, p3, tied, e0, e1, e2, e3, total_ref):
    _, local, _ = place()
    pieces = [p[...] for p in (p0, p1, p2, p3)]
    chips = [local ^ s for s in range(4)]
    for s, e in enumerate((e0, e1, e2, e3)):
        acc = jnp.zeros((PIECE, HEAD_DIM), jnp.float32)
        for o in range(4):
            if o != s:
                acc = acc + jnp.where(chips[o] < chips[s], pieces[o], 0.0)
        e[...] = acc
    total_ref[...] = (pieces[0] + pieces[1]) + (pieces[2] + pieces[3])


def across_groups(bit, e0, e1, e2, e3, total_ref, got_ref, tied, f0, f1, f2, f3, *sum_ref):
    _, _, group = place()
    got = got_ref[...]
    earlier = jnp.where((group & bit) != 0, got, 0.0)
    for e, f in zip((e0, e1, e2, e3), (f0, f1, f2, f3)):
        f[...] = e[...] + earlier
    for ref in sum_ref:
        ref[...] = total_ref[...] + got


def both_cores(b0, b1, b2, b3, keep_ref, got_ref, tied, mine_ref, send_ref):
    core, _, _ = place()
    for s, b in enumerate((b0, b1, b2, b3)):
        before = b[...]
        mine_ref[s] = before + jnp.where(core == 1, got_ref[s], 0.0)
        send_ref[s] = before + jnp.where(core == 0, keep_ref[s], 0.0)


def per_device(queries, keys, values):
    rows = queries.shape[0]
    count = rows // SPAN
    devices_n = lax.axis_size("block")
    groups_n = devices_n // 8
    assert groups_n * 8 == devices_n and groups_n & (groups_n - 1) == 0

    f32, bf16 = jnp.float32, jnp.bfloat16
    sds = jax.ShapeDtypeStruct

    state_shapes = (
        sds((HALF, rows, HEAD_DIM), bf16),
        sds((HALF, rows, HEAD_DIM), f32),
        sds((HALF, (count + 7) // 8 * 8, HEAD_DIM), f32),
        sds((HALF, PIECE, HEAD_DIM), f32),
    )
    query_shapes = (
        sds((HALF, rows, 2 * HEAD_DIM), bf16),
        sds((HALF, rows, HEAD_DIM), f32),
    )
    token = sds((8, HEAD_DIM), f32)
    half_flops = HALF * count * 2 * SPAN * HEAD_DIM * HEAD_DIM

    def call(kernel, ins, outs, in_specs=None, out_specs=None, grant=8, flops=half_flops, nbytes=8 << 20, **more):
        return pl.pallas_call(
            kernel,
            out_shape=outs,
            in_specs=in_specs or [VM] * len(ins),
            out_specs=out_specs or (VM,) * len(outs),
            compiler_params=pltpu.CompilerParams(vmem_limit_bytes=grant << 20),
            cost_estimate=pl.CostEstimate(flops=flops, bytes_accessed=nbytes, transcendentals=0),
            **more,
        )(*ins)

    def small(kernel, ins, outs):
        return call(kernel, ins, outs, flops=1 << 20, nbytes=1 << 19)

    def swap(x, distance):
        return lax.ppermute(x, "block", [(i, i ^ distance) for i in range(devices_n)])

    def swap_slot(x, slot):
        return swap(x, 2 * slot)

    k_vm, v_vm, fk_a, pf_a, nf_a, t_send = call(
        functools.partial(pre_a, count),
        (keys, values),
        (sds((HEADS, rows, HEAD_DIM), bf16),) * 2 + state_shapes,
        in_specs=[HBM, HBM],
        grant=42,
        scratch_shapes=[pltpu.SemaphoreType.DMA((2, HEADS, READS))],
    )
    t_got = swap(t_send, 1)
    fk_b, pf_b, nf_b, t_keep = call(functools.partial(pre_b, count), (k_vm, v_vm), state_shapes)

    piece = sds((PIECE, HEAD_DIM), f32)

    pieces = small(add_totals, (t_keep, t_got), (piece,) * 4)
    landed = {}
    for s in SLOT_ORDER:
        landed[s] = swap_slot(pieces[s], s)
    fqs_b, den_b, done_b = call(
        functools.partial(mid_mine, count), (queries, fk_b, nf_b), (*query_shapes, token)
    )
    *finals, total = small(
        inside_group, (pieces[0], landed[1], landed[2], landed[3], done_b), (piece,) * 5
    )
    fqs_a, den_a, done_a = call(
        functools.partial(mid_other, count), (queries, fk_a, nf_a), (*query_shapes, token)
    )
    bit = 1
    while bit < groups_n:
        got = swap(total, 8 * bit)
        sums = 1 if 2 * bit < groups_n else 0
        finals = small(
            functools.partial(across_groups, bit),
            (*finals[:4], total, got, done_a),
            (piece,) * (4 + sums),
        )
        total = finals[-1]
        bit *= 2
    back = {0: finals[0]}
    for s in SLOT_ORDER:
        back[s] = swap_slot(finals[s], s)
    half_out = sds((rows, HALF * HEAD_DIM), bf16)
    first, done_first = call(
        functools.partial(post_first, count),
        (fqs_b, den_b, v_vm, finals[0], t_got, pf_b),
        (half_out, token),
        scratch_shapes=[pltpu.VMEM((1, PIECE, HEAD_DIM), f32)],
    )
    four = sds((HALF, PIECE, HEAD_DIM), f32)
    before_b, send_a = small(
        both_cores, (back[0], back[1], back[2], back[3], t_keep, t_got, done_first), (four, four)
    )
    before_a = swap(send_a, 1)

    (mine,) = call(
        functools.partial(post_mine, count),
        (fqs_b, den_b, v_vm, before_b, pf_b, first),
        (half_out,),
        input_output_aliases={5: 0},
    )
    return call(
        functools.partial(post_other, count),
        (fqs_a, den_a, v_vm, before_a, pf_a, mine),
        sds((rows, HEADS * HEAD_DIM), bf16),
        out_specs=HBM,
        scratch_shapes=[
            pltpu.VMEM((rows, HALF * HEAD_DIM), bf16),
            pltpu.SemaphoreType.DMA((2, count)),
        ],
    )


def solution(mesh):
    placed = P(("groups", "block"), None)

    return jax.shard_map(
        per_device,
        mesh=mesh,
        in_specs=(placed, placed, placed),
        out_specs=placed,
        check_vma=False,
    )
```
